32 devices in a mesh: row: 4 (over z), col: 8 (over y, x, core).
Axes of the slice: x: 2, y: 2, z: 4, core: 2. Of those that a mesh axis runs over, the one named last changes fastest.
Arguments:
- covariance: float32 [16384, 16384], P('row', 'col'), may hold values from -1 to 3, as said below
- center: float32 [16384], replicated, may hold values from 0.4 to 1
- links: float32 [4, 16384], replicated, may hold values from 0.05 to 0.25
- process: float32 [16384], replicated, may hold values from 0.1 to 1
- wells: int32 [1, 256], replicated, may hold values from 0 to 16383, as said below
- noise: float32 [1, 256], replicated, may hold values from 0.05 to 0.5
Outputs:
- updated: float32 [16384, 16384], P('row', 'col')
The draws below stay inside these ranges and needn't reach their ends.
Inputs may be any that keep to these rules, and one draw needn't show every extreme that they name: `covariance`: symmetric positive definite. `wells`: each row holds 256 distinct cells; at most 32 of them lie in one aligned block of 2048 cells, and exactly 32 in some block.
All inputs are finite; a program needn't handle non-finite values.
Results may differ from the reference program's by a relative error of at most 0.0001.
Values sent between devices are 32-bit elements; how exact they have to be, the bound alone decides.
A program may use at most 320 MiB of HBM per device.

```python
import math
import jax
import jax.numpy as jnp
from jax import lax

NGX = 128
NGY = 128
M = 256
WMAX = 32
STEPS = 1
NCELL = 16384
CBLK = 2048


def draw_covariance(key, part):
    base = jax.random.normal(key, (NCELL, NCELL), jnp.float32)
    lift = 2.0
    sym = (base + base.T) * (0.5 / math.sqrt(NCELL))
    return sym + lift * jnp.eye(NCELL, dtype=jnp.float32)


def draw_wells(key, part):
    blocks = NCELL // CBLK
    keys = jax.random.split(jax.random.fold_in(key, 11), STEPS * blocks)
    perms = jax.vmap(lambda k: jax.random.permutation(k, CBLK))(keys).reshape(STEPS, blocks, CBLK)
    first = jax.random.randint(jax.random.fold_in(key, 12), (STEPS,), 0, blocks)
    slot = jnp.arange(M, dtype=jnp.int32)
    later = jnp.maximum(slot - WMAX, 0)
    span = max(blocks - 1, 1)
    block = jnp.where(slot[None, :] < WMAX, first[:, None], (first[:, None] + 1 + later[None, :] % span) % blocks)
    rank = jnp.where(slot[None, :] < WMAX, slot[None, :], later[None, :] // span)
    offset = perms[jnp.arange(STEPS, dtype=jnp.int32)[:, None], block, rank]
    cells = (block * CBLK + offset).astype(jnp.int32)
    orders = jax.vmap(lambda k: jax.random.permutation(k, M))(jax.random.split(jax.random.fold_in(key, 13), STEPS))
    return jnp.take_along_axis(cells, orders.astype(jnp.int32), axis=1).astype(jnp.int32)


def setup_inputs(seed: int = 0) -> dict:
    arg_keys = jax.random.split(jax.random.key(seed), 7)
    covariance = draw_covariance(jax.random.fold_in(arg_keys[6], 71), 0)
    center = jnp.clip(jnp.exp(jax.random.uniform(arg_keys[1], (NCELL,), jnp.float32, math.log(0.4), math.log(1.0))), 0.4, 1.0)
    links = jnp.clip(jnp.exp(jax.random.uniform(arg_keys[2], (4, NCELL), jnp.float32, math.log(0.05), math.log(0.25))), 0.05, 0.25)
    process = jnp.clip(jnp.exp(jax.random.uniform(arg_keys[3], (NCELL,), jnp.float32, math.log(0.1), math.log(1.0))), 0.1, 1.0)
    wells = draw_wells(jax.random.fold_in(arg_keys[6], 71), 0)
    noise = jnp.clip(jnp.exp(jax.random.uniform(arg_keys[5], (STEPS, M), jnp.float32, math.log(0.05), math.log(0.5))), 0.05, 0.5)
    return dict(covariance=covariance, center=center, links=links, process=process, wells=wells, noise=noise)


def apply_left(matrix, center, links):
    field = matrix.reshape(NGX, NGY, -1)
    padded = jnp.pad(field, ((1, 1), (1, 1), (0, 0)))
    own = center.reshape(NGX, NGY, 1)
    coef = links.reshape(4, NGX, NGY, 1)
    out = own * field + coef[0] * padded[:-2, 1:-1] + coef[1] * padded[2:, 1:-1]
    out = out + coef[2] * padded[1:-1, :-2] + coef[3] * padded[1:-1, 2:]
    return out.reshape(NCELL, -1)

def apply_right(matrix, center, links):
    field = matrix.reshape(-1, NGX, NGY)
    padded = jnp.pad(field, ((0, 0), (1, 1), (1, 1)))
    own = center.reshape(1, NGX, NGY)
    coef = links.reshape(4, 1, NGX, NGY)
    out = own * field + coef[0] * padded[:, :-2, 1:-1] + coef[1] * padded[:, 2:, 1:-1]
    out = out + coef[2] * padded[:, 1:-1, :-2] + coef[3] * padded[:, 1:-1, 2:]
    return out.reshape(-1, NCELL)

def reference(covariance, center, links, process, wells, noise):
    current = covariance
    diag_index = jnp.arange(NCELL, dtype=jnp.int32)
    for step in range(STEPS):
        left = apply_left(current, center, links)
        predicted = apply_right(left, center, links)
        predicted = predicted.at[diag_index, diag_index].add(process)
        chosen = wells[step]
        strip = jnp.take(predicted, chosen, axis=1)
        across = jnp.take(predicted, chosen, axis=0)
        innovation = jnp.take(strip, chosen, axis=0) + jnp.diag(noise[step])
        factor = jnp.linalg.cholesky(innovation)
        solved = jax.scipy.linalg.cho_solve((factor, True), across)
        current = predicted - jnp.dot(strip, solved, precision=lax.Precision.HIGHEST)
    return current
```

```python
import jax
import jax.numpy as jnp
from jax import lax
from jax.experimental import pallas as pl
from jax.experimental.pallas import tpu as pltpu
from jax.sharding import PartitionSpec as P

NGY = 128
WMAX = 32
HIGHEST = lax.Precision.HIGHEST


def stencil_kernel(base_ref, x_ref, top_ref, bot_ref, lh_ref, rh_ref, crow_ref, ccol_ref, o_ref, ring, left, cb):
    i = pl.program_id(0)
    steps = pl.num_programs(0)
    cols = x_ref.shape[1]
    tiles = cols // NGY

    def put(slot, body, ext):
        rows = pl.ds(pl.multiple_of(ext * NGY, NGY), NGY)
        ring[slot, :, :NGY] = lh_ref[rows, :]
        ring[slot, :, NGY : NGY + cols] = body[...]
        ring[slot, :, NGY + cols :] = rh_ref[rows, :]

    now = lax.rem(i, 3)

    @pl.when(i == 0)
    def _():
        put(2, top_ref, 0)

    @pl.when(i < steps - 1)
    def _():
        put(now, x_ref, i + 1)

    @pl.when(i == steps - 1)
    def _():
        put(now, bot_ref, i + 1)

    @pl.when(i > 0)
    def _():
        mid = lax.rem(i + 2, 3)
        old = lax.rem(i + 1, 3)
        for c in range(5):
            cb[c] = jnp.broadcast_to(crow_ref[:, c : c + 1], (NGY, NGY))
        for k in range(tiles + 2):
            at = slice(k * NGY, (k + 1) * NGY)
            x = ring[mid, :, at]
            acc = cb[0] * x + cb[1] * ring[old, :, at] + cb[2] * ring[now, :, at]
            acc = acc + cb[3] * pltpu.roll(x, 1, 0) + cb[4] * pltpu.roll(x, NGY - 1, 0)
            left[:, at] = acc
        for k in range(tiles):
            at = slice(k * NGY, (k + 1) * NGY)
            x = left[:, (k + 1) * NGY : (k + 2) * NGY]
            acc = ccol_ref[0:1, at] * x + ccol_ref[1:2, at] * left[:, at]
            acc = acc + ccol_ref[2:3, at] * left[:, (k + 2) * NGY : (k + 3) * NGY]
            acc = acc + ccol_ref[3:4, at] * pltpu.roll(x, 1, 1)
            acc = acc + ccol_ref[4:5, at] * pltpu.roll(x, NGY - 1, 1)
            o_ref[:, at] = acc
        d0 = base_ref[0] + (i - 1) * NGY

        @pl.when((d0 >= 0) & (d0 < cols))
        def _():
            r = lax.broadcasted_iota(jnp.int32, (NGY, NGY), 0)
            c = lax.broadcasted_iota(jnp.int32, (NGY, NGY), 1)
            noise = jnp.broadcast_to(crow_ref[:, 5:6], (NGY, NGY))
            at = pl.ds(pl.multiple_of(d0, NGY), NGY)
            o_ref[:, at] = o_ref[:, at] + jnp.where(r == c, noise, 0.0)


def stencil(base, cov, top, bot, lh, rh, crow, ccol):
    rows, cols = cov.shape
    grid = rows // NGY
    whole = lambda a: pl.BlockSpec(a.shape, lambda i: (0, 0))
    return pl.pallas_call(
        stencil_kernel,
        grid=(grid + 1,),
        in_specs=[
            pl.BlockSpec(memory_space=pltpu.SMEM),
            pl.BlockSpec((NGY, cols), lambda i: (jnp.minimum(i, grid - 1), 0)),
            whole(top),
            whole(bot),
            whole(lh),
            whole(rh),
            pl.BlockSpec((NGY, 8), lambda i: (jnp.maximum(i - 1, 0), 0)),
            whole(ccol),
        ],
        out_specs=pl.BlockSpec((NGY, cols), lambda i: (jnp.maximum(i - 1, 0), 0)),
        out_shape=jax.ShapeDtypeStruct((rows, cols), jnp.float32),
        scratch_shapes=[
            pltpu.VMEM((3, NGY, cols + 2 * NGY), jnp.float32),
            pltpu.VMEM((NGY, cols + 2 * NGY), jnp.float32),
            pltpu.VMEM((5, NGY, NGY), jnp.float32),
        ],
        compiler_params=pltpu.CompilerParams(vmem_limit_bytes=40 * 1024 * 1024),
        cost_estimate=pl.CostEstimate(
            flops=18 * rows * cols, bytes_accessed=8 * rows * cols, transcendentals=0
        ),
        name="stencil",
    )(base, cov, top, bot, lh, rh, crow, ccol)


def coefficients(center, links, start, count):
    cells = jnp.arange(count, dtype=jnp.int32) % NGY
    own = lax.dynamic_slice_in_dim(center, start, count)
    link = lax.dynamic_slice_in_dim(links, start, count, 1)
    return [
        own,
        link[0],
        link[1],
        jnp.where(cells == 0, 0.0, link[2]),
        jnp.where(cells == NGY - 1, 0.0, link[3]),
    ]


def shards(covariance, center, links, process, wells, noise):
    row_id = lax.axis_index("row")
    col_id = lax.axis_index("col")
    nrow = lax.axis_size("row")
    ncol = lax.axis_size("col")
    rows, cols = covariance.shape
    ratio = rows // cols
    row_start = row_id * rows
    col_start = col_id * cols

    up = lambda n: [(j, j + 1) for j in range(n - 1)]
    down = lambda n: [(j + 1, j) for j in range(n - 1)]
    top = lax.ppermute(covariance[-NGY:], "row", up(nrow))
    bot = lax.ppermute(covariance[:NGY], "row", down(nrow))
    lh = lax.ppermute(covariance[:, -NGY:], "col", up(ncol))
    rh = lax.ppermute(covariance[:, :NGY], "col", down(ncol))
    lc = lax.ppermute(jnp.concatenate([top[:, -NGY:], bot[:, -NGY:]]), "col", up(ncol))
    rc = lax.ppermute(jnp.concatenate([top[:, :NGY], bot[:, :NGY]]), "col", down(ncol))
    lh = jnp.concatenate([lc[:NGY], lh, lc[NGY:]])
    rh = jnp.concatenate([rc[:NGY], rh, rc[NGY:]])

    noise_rows = lax.dynamic_slice_in_dim(process, row_start, rows)
    crow = coefficients(center, links, row_start, rows) + [noise_rows]
    crow = jnp.stack(crow + [jnp.zeros_like(noise_rows)] * 2, axis=1)
    ccol = coefficients(center, links, col_start, cols)
    ccol = jnp.stack(ccol + [jnp.zeros_like(ccol[0])] * 3, axis=0)
    base = jnp.reshape(row_start - col_start, (1,)).astype(jnp.int32)
    predicted = stencil(base, covariance, top, bot, lh, rh, crow, ccol)

    chosen = wells[0]
    block = chosen // cols
    ahead = (block[None, :] == block[:, None]) & (chosen[None, :] < chosen[:, None])
    slot = block * WMAX + jnp.sum(ahead.astype(jnp.int32), axis=1)
    slots = ncol * WMAX
    onehot = slot[None, :] == jnp.arange(slots, dtype=jnp.int32)[:, None]
    valid = jnp.any(onehot, axis=1)
    cell = jnp.sum(jnp.where(onehot, chosen[None, :], 0), axis=1)
    noise_slot = jnp.sum(jnp.where(onehot, noise[0][None, :], 0.0), axis=1)

    mine = ratio * WMAX
    row_cell = lax.dynamic_slice_in_dim(cell, row_id * mine, mine)
    row_valid = lax.dynamic_slice_in_dim(valid, row_id * mine, mine)
    row_local = jnp.clip(row_cell - row_start, 0, rows - 1)
    part = jnp.where(row_valid[:, None], jnp.take(predicted, row_local, axis=0, mode="clip"), 0.0)

    col_cell = lax.dynamic_slice_in_dim(cell, col_id * WMAX, WMAX)
    col_valid = lax.dynamic_slice_in_dim(valid, col_id * WMAX, WMAX)
    pick = (jnp.arange(cols, dtype=jnp.int32)[:, None] == (col_cell - col_start)[None, :]) & col_valid[None, :]
    gram = jnp.dot(part, pick.astype(jnp.float32), precision=HIGHEST)
    gram = lax.all_gather(gram, "col", axis=1, tiled=True)
    gram = lax.all_gather(gram, "row", axis=0, tiled=True)

    across = lax.all_gather(part, "row", axis=0, tiled=True)

    pieces = []
    for j in range(ratio):
        perm = []
        for r in range(nrow):
            for c in range(ncol):
                to_row = c // ratio
                to_col = r * ratio + (j + c) % ratio
                perm.append((r * ncol + c, to_row * ncol + to_col))
        sub = lax.rem(j + col_id, ratio)
        sent = lax.dynamic_slice_in_dim(part, sub * WMAX, WMAX)
        pieces.append(lax.ppermute(sent, ("row", "col"), perm))
    pieces = jnp.stack(pieces)
    ordered = [
        lax.dynamic_index_in_dim(pieces, lax.rem(col_id - q + ratio * ncol, ratio), 0, keepdims=False)
        for q in range(ratio)
    ]
    strip = lax.all_gather(jnp.concatenate(ordered, axis=1), "col", axis=0, tiled=True)

    innovation = gram + jnp.diag(jnp.where(valid, noise_slot, 1.0))
    factor = jnp.linalg.cholesky(innovation, symmetrize_input=False)
    inverse = lax.linalg.triangular_solve(
        factor, jnp.eye(slots, dtype=jnp.float32), left_side=True, lower=True
    )
    solved = jnp.dot(inverse.T, jnp.dot(inverse, across, precision=HIGHEST), precision=HIGHEST)
    update = lax.dot_general(
        strip, solved, (((0,), (0,)), ((), ())), precision=lax.Precision.HIGH
    )
    return predicted - update


def solution(mesh):
    in_specs = (P("row", "col"), P(), P(), P(), P(), P())
    out_specs = P("row", "col")
    return jax.shard_map(shards, mesh=mesh, in_specs=in_specs, out_specs=out_specs, check_vma=False)
```
